32 devices in a mesh: obs: 8 (over z, core), coef: 4 (over y, x).
Axes of the slice: x: 2, y: 2, z: 4, core: 2. Of those that a mesh axis runs over, the one named last changes fastest.
Arguments:
- design: bfloat16 [256, 5120], P('obs', 'coef'), may hold values from -6 to 6
- filter_taps: float32 [128], replicated, may hold values from -0.5 to 0.5
- valid_counts: int32 [8], P('obs'), may hold values from 16 to 32
Outputs:
- normal: float32 [5120, 5120], P('obs', 'coef')
The draws below stay inside these ranges and needn't reach their ends.
Inputs may be any that keep to these rules, and one draw needn't show every extreme that they name: `valid_counts`: number of leading valid times in each block of 32 consecutive times.
All inputs are finite; a program needn't handle non-finite values.
Results may differ from the reference program's by a relative error of at most 0.0029.
Values may be sent and summed in bfloat16 or wider, within the bound.
No kernel may reach another device: no remote copies, remote signals or barrier semaphores. Data moves between devices by JAX's collectives and lax.ppermute only.
A program may use at most 64 MiB of HBM per device.

```python
import jax
import jax.numpy as jnp
from jax import lax

ROWS_DEV = 32
TAPS = 128
TIME = 256
COLS = 5120
BLOCKS = 8


def place_ends(entries, key, low, high):
    longest = entries.shape.index(max(entries.shape))
    spots = []
    for shift in (0, 1):
        where = [jax.random.randint(jax.random.fold_in(key, axis), (), 0, length) for axis, length in enumerate(entries.shape)]
        where[longest] = (where[longest] + shift) % entries.shape[longest]
        spots.append(tuple(where))
    return entries.at[spots[0]].set(low).at[spots[1]].set(high)


def shard_levels(rng, shape, split, least, largest):
    gain, own = 1.0, jax.random.fold_in(rng, 6)
    for position, blocks in split:
        steps = jnp.exp(jax.random.uniform(jax.random.fold_in(own, position), (blocks,), jnp.float32, least / len(split), largest / len(split)))
        gain = gain * jnp.repeat(steps, shape[position] // blocks).reshape([-1 if axis == position else 1 for axis in range(len(shape))])
    return gain


def bell_draw(rng, extent, spread, limit, split=(), kind=jnp.bfloat16):
    level = shard_levels(rng, extent, split, -0.22, 0.18) if split else 1.0
    drawn = jax.random.normal(rng, extent, jnp.float32) * spread * level
    return jnp.minimum(jnp.maximum(drawn, -limit), limit).astype(kind)


def setup_inputs(seed: int = 0) -> dict:
    arg_keys = jax.random.split(jax.random.key(seed), 4)
    return {
        "design": bell_draw(arg_keys[0], (TIME, COLS), 1.0, 6.0, ((0, 8), (1, 4))),
        "filter_taps": bell_draw(arg_keys[1], (TAPS,), 0.0884, 0.5, (), jnp.float32),
        "valid_counts": place_ends(jax.random.randint(arg_keys[2], (BLOCKS,), ROWS_DEV // 2, ROWS_DEV + 1), jax.random.fold_in(arg_keys[2], 1), ROWS_DEV // 2, ROWS_DEV).astype(jnp.int32),
    }


def tap_matrix(filter_taps, out_rows, span):
    row_index = jnp.arange(out_rows, dtype=jnp.int32)[:, None]
    col_index = jnp.arange(span, dtype=jnp.int32)[None, :]
    lag_index = row_index + TAPS - col_index
    inside = (lag_index >= 0) & (lag_index < TAPS)
    values = jnp.take(filter_taps, jnp.clip(lag_index, 0, TAPS - 1))
    return jnp.where(inside, values, jnp.zeros_like(values))


def reference(design, filter_taps, valid_counts):
    n_time = design.shape[0]
    block_rows = 128 if n_time % 128 == 0 else n_time
    padded = jnp.concatenate([jnp.zeros((TAPS, design.shape[1]), jnp.float32), design.astype(jnp.float32)], 0)
    matrix = tap_matrix(filter_taps, block_rows, block_rows + TAPS)

    def one_block(block_number):
        start = (block_number * block_rows).astype(jnp.int32)
        window = lax.dynamic_slice_in_dim(padded, start, block_rows + TAPS, 0)
        return jnp.dot(matrix, window, precision=lax.Precision.HIGHEST)

    filtered = lax.map(one_block, jnp.arange(n_time // block_rows, dtype=jnp.int32)).reshape(n_time, -1)
    local_time = jnp.arange(n_time, dtype=jnp.int32) % ROWS_DEV
    row_mask = (local_time < jnp.repeat(valid_counts, ROWS_DEV)).astype(jnp.float32)
    weighted = (filtered * row_mask[:, None]).astype(jnp.bfloat16)
    wide = weighted.astype(jnp.float32)
    normal = lax.dot_general(wide, wide, (((0,), (0,)), ((), ())), precision=lax.Precision.HIGHEST)
    return normal * (1.0 / n_time)
```

```python
import jax
import jax.numpy as jnp
from jax import lax
from jax.experimental import pallas as pl
from jax.experimental.pallas import tpu as pltpu
from jax.sharding import PartitionSpec as P

LANES = 128
AXES = ("obs", "coef")


def far_partner(distance, count):
    width = count.bit_length() - 1
    back = 0
    for bit in range(width):
        if distance >> bit & 1:
            back |= 1 << (width - 1 - bit)
    return (count - 1) ^ back


def row_tile(rows):
    for tile in (128, 112, 96, 80, 64, 48, 32, 16):
        if rows % tile == 0:
            return tile
    return rows


def filter_row(filter_taps):
    taps = filter_taps.shape[0]
    return jnp.concatenate(
        [jnp.zeros((1,), jnp.float32), filter_taps[::-1], jnp.zeros((taps - 1,), jnp.float32)]
    ).reshape(1, 2 * taps)


def bf16_parts(value):
    high = value.astype(jnp.bfloat16)
    rest = value - high.astype(jnp.float32)
    middle = rest.astype(jnp.bfloat16)
    low = (rest - middle.astype(jnp.float32)).astype(jnp.bfloat16)
    return high, middle, low


def assemble(copies, sem):
    started = []
    for source, target in copies:
        started.append(pltpu.make_async_copy(source, target, sem.at[len(started)]))
        started[-1].start()
    for copy in started:
        copy.wait()


def make_kernel(loader, n_time, n_rows, n_cols, block_rows, taps, tile, n_refs):
    scale = 1.0 / n_time
    width = min(n_cols, 256)

    def filtered(parts, raw, start, left, size):
        total = None
        for part in reversed(parts):
            if start == 0:
                part, first = part[:, taps:], 0
            else:
                first = start - taps
            term = jnp.dot(
                part,
                raw[first : start + taps, left : left + size],
                preferred_element_type=jnp.float32,
            )
            total = term if total is None else total + term
        return total

    def kernel(row_ref, *refs):
        ins, out_ref = refs[:n_refs], refs[n_refs]
        raw_a, raw_b, side_a, side_b, sem = refs[n_refs + 1 :]

        @pl.when(pl.program_id(0) == 0)
        def _():
            loader(ins, raw_a, raw_b, sem)
            wide = jnp.broadcast_to(row_ref[...], (taps, 2 * taps))
            matrix = pltpu.roll(wide, 0, 1, stride=1, stride_axis=0)
            parts = bf16_parts(matrix)
            for start in range(0, n_time, taps):
                rows = pl.ds(start, taps)
                local = lax.broadcasted_iota(jnp.int32, (taps, LANES), 0) % block_rows
                count = raw_b[rows, n_cols : n_cols + LANES].astype(jnp.float32)
                keep = (local.astype(jnp.float32) < count).astype(jnp.float32)
                for left in range(0, n_cols, width):
                    value = filtered(parts, raw_b, start, left, width)
                    value = value * jnp.concatenate([keep] * (width // LANES), 1)
                    side_b[rows, left : left + width] = value.astype(jnp.bfloat16)
                step = 128 if n_rows % 128 == 0 else n_rows
                for left in range(0, n_rows, step):
                    value = filtered(parts, raw_a, start, left, step)
                    side_a[left : left + step, rows] = value.T.astype(jnp.bfloat16)

        top = pl.multiple_of(pl.program_id(0) * tile, tile)
        out_ref[...] = scale * jnp.dot(
            side_a[pl.ds(top, tile), :], side_b[...], preferred_element_type=jnp.float32
        )

    return kernel


def assembled_normal(filter_taps, arrays, loader, n_time, n_rows, n_cols, block_rows):
    taps = filter_taps.shape[0]
    tile = row_tile(n_rows)
    raw_rows_width = -(-n_rows // LANES) * LANES
    kernel = make_kernel(loader, n_time, n_rows, n_cols, block_rows, taps, tile, len(arrays))
    return pl.pallas_call(
        kernel,
        grid=(n_rows // tile,),
        out_shape=jax.ShapeDtypeStruct((n_rows, n_cols), jnp.float32),
        in_specs=[pl.BlockSpec(memory_space=pltpu.VMEM)]
        + [pl.BlockSpec(memory_space=pl.ANY)] * len(arrays),
        out_specs=pl.BlockSpec((tile, n_cols), lambda i: (i, 0)),
        scratch_shapes=[
            pltpu.VMEM((n_time, raw_rows_width), jnp.bfloat16),
            pltpu.VMEM((n_time, n_cols + LANES), jnp.bfloat16),
            pltpu.VMEM((n_rows, n_time), jnp.bfloat16),
            pltpu.VMEM((n_time, n_cols), jnp.bfloat16),
            pltpu.SemaphoreType.DMA((2 * len(arrays) + 2,)),
        ],
        cost_estimate=pl.CostEstimate(
            flops=2 * n_time * n_rows * n_cols,
            bytes_accessed=4 * n_rows * n_cols,
            transcendentals=0,
        ),
    )(filter_row(filter_taps), *arrays)


def counts_beside(rows, counts):
    return jnp.broadcast_to(counts.astype(jnp.bfloat16)[:, None], (rows, LANES))


def permuted_plan(design, filter_taps, valid_counts):
    block_rows, n_cols = design.shape
    coef_count = lax.axis_size("coef")
    n_rows = n_cols // 2
    n_time = 2 * coef_count * block_rows
    span = 2 * block_rows

    def place(chip, core, column):
        return (2 * chip + core) * coef_count + column

    def send(value, pairs):
        return lax.ppermute(value, AXES, [(place(*a), place(*b)) for a, b in pairs])

    chips = range(coef_count)
    both = [(z, h, c) for z in chips for h in (0, 1) for c in chips]
    swap = [((z, h, c), (z, 1 - h, c)) for z, h, c in both]
    other = send(design, swap)
    other_count = send(valid_counts, swap)
    packed = jnp.concatenate(
        [
            jnp.concatenate([design, other], 0),
            jnp.concatenate(
                [counts_beside(block_rows, valid_counts), counts_beside(block_rows, other_count)], 0
            ),
        ],
        1,
    )
    spread = send(
        packed,
        [
            ((z, 1, t), (t, 1, t ^ far_partner(t ^ z, coef_count)))
            for z in chips
            for t in chips
        ],
    )
    column_blocks, row_blocks = [packed], [spread]
    for flip in range(1, coef_count):
        column_blocks.append(
            send(packed, [((z, 0, c), (z ^ flip, 0, c)) for z in chips for c in chips])
        )
    for flip in range(1, coef_count):
        row_blocks.append(
            send(spread, [((z, 1, c), (z, 1, c ^ flip)) for z in chips for c in chips])
        )
    column_over = [send(v, [((z, 0, c), (z, 1, c)) for z in chips for c in chips]) for v in column_blocks]
    row_over = [send(v, [((z, 1, c), (z, 0, c)) for z in chips for c in chips]) for v in row_blocks]
    arrays = column_blocks + column_over + row_blocks + row_over
    n = coef_count

    def far(distance):
        value = jnp.int32(0)
        for d in range(n):
            value = jnp.where(distance == d, jnp.int32(far_partner(d, n)), value)
        return value

    def loader(ins, raw_a, raw_b, sem):
        me, column = lax.axis_index("obs"), lax.axis_index("coef")
        chip, core = me // 2, me % 2

        def copies(columns, rows):
            left = pl.multiple_of(core * n_rows, LANES)
            todo = []
            for flip in range(n):
                top = pl.multiple_of((chip ^ flip) * span, span)
                todo.append((columns[flip], raw_b.at[pl.ds(top, span), :]))
            for flip in range(n):
                source = chip ^ far((column ^ flip) ^ chip)
                top = pl.multiple_of(source * span, span)
                for part in (0, 1):
                    todo.append(
                        (
                            rows[flip].at[pl.ds((1 - part) * block_rows, block_rows), pl.ds(left, n_rows)],
                            raw_a.at[pl.ds(top + part * block_rows, block_rows), :],
                        )
                    )
            return todo

        @pl.when(core == 0)
        def _():
            assemble(copies(ins[:n], ins[3 * n :]), sem)

        @pl.when(core == 1)
        def _():
            assemble(copies(ins[n : 2 * n], ins[2 * n : 3 * n]), sem)

    return assembled_normal(
        filter_taps, arrays, loader, n_time, n_rows, n_cols, block_rows
    )


def gathered_plan(design, filter_taps, valid_counts):
    block_rows, n_cols = design.shape
    obs_count, coef_count = lax.axis_size("obs"), lax.axis_size("coef")
    group = obs_count // coef_count
    n_rows = n_cols // group
    n_time = obs_count * block_rows
    packed = jnp.concatenate([design, counts_beside(block_rows, valid_counts)], 1)
    columns = lax.all_gather(packed, "obs", axis=0, tiled=True)
    my_slot = lax.axis_index("obs") % group
    halves = []
    for shift in range(group):
        slot = (my_slot + shift) % group
        piece = lax.dynamic_slice_in_dim(design, slot * n_rows, n_rows, 1)
        pairs = []
        for a in range(coef_count):
            for s in range(group):
                for t in range(coef_count):
                    pairs.append(
                        (
                            (a * group + s) * coef_count + t,
                            (t * group + (s + shift) % group) * coef_count + a,
                        )
                    )
        halves.append(lax.ppermute(piece, AXES, pairs))
    stacked = jnp.stack(halves)
    order = (my_slot - jnp.arange(group)) % group
    mine = stacked[order].reshape(group * block_rows, n_rows)
    rows = lax.all_gather(mine, "coef", axis=0, tiled=True)
    pad = -n_rows % LANES
    if pad:
        rows = jnp.pad(rows, ((0, 0), (0, pad)))

    def loader(ins, raw_a, raw_b, sem):
        assemble([(ins[0], raw_b), (ins[1], raw_a)], sem)

    return assembled_normal(
        filter_taps, [columns, rows], loader, n_time, n_rows, n_cols, block_rows
    )


def solution(mesh):
    obs_count, coef_count = mesh.shape["obs"], mesh.shape["coef"]
    small = obs_count == 2 * coef_count and coef_count in (2, 4)
    plan = permuted_plan if small else gathered_plan
    return jax.shard_map(
        plan,
        mesh=mesh,
        in_specs=(P("obs", "coef"), P(), P("obs")),
        out_specs=P("obs", "coef"),
        check_vma=False,
    )
```
